32 devices in a mesh: groups: 2 (over y), hid: 4 (over z), rows: 2 (over x), mp: 2 (over core).
Axes of the slice: x: 2, y: 2, z: 4, core: 2. Of those that a mesh axis runs over, the one named last changes fastest.
Arguments:
- tokens: bfloat16 [1024, 4096], P(('groups', 'rows'), 'hid'), parts along dimension 0, may hold values from -6 to 6
- norm_gain: float32 [2, 4096], P('mp'), may hold values from 0.1 to 1.9
- gate_weight: bfloat16 [2, 4096, 14336], P('mp', 'rows', 'hid'), may hold values from -0.09375 to 0.09375
- up_weight: bfloat16 [2, 4096, 14336], P('mp', 'rows', 'hid'), may hold values from -0.09375 to 0.09375
- down_weight: bfloat16 [2, 14336, 4096], P('mp', 'hid', 'rows'), may hold values from -0.046875 to 0.046875
- enc_weight: bfloat16 [2, 4096, 16384], P('mp', 'rows', 'hid'), may hold values from -0.0625 to 0.0625
- enc_bias: float32 [16384], P('hid'), may hold values from -3 to 3
- adjoint: bfloat16 [1024, 16384], P(('groups', 'rows', 'mp'), 'hid'), parts along dimension 0, may hold values from -6 to 6
Outputs:
- gated: bfloat16 [1024, 16384], P(('groups', 'rows', 'mp'), 'hid'), parts along dimension 0
The draws below stay inside these ranges and needn't reach their ends.
There are 2 independent parts, one for each index of `groups`. The reference program is written for one: setup_inputs(seed, part) draws one part's arguments, and reference() takes and returns one part's arrays. A program takes and returns all parts, laid end to end along the dimension named above; an argument that names none is the same for every part. Nothing has to cross between parts.
All inputs are finite; a program needn't handle non-finite values.
Results may differ from the reference program's by a relative error of at most 0.0058.
Values may be sent and summed in bfloat16 or wider, within the bound.
A program may use at most 128 MiB of HBM per device.

```python
import jax
import jax.numpy as jnp
from jax import lax

D = 4096
FF = 14336
FEATURES = 16384
TOKENS = 512


def levels(stream_key, dims, split, smallest, top_value):
    def one(axis_at, shards_of):
        steps = jax.random.uniform(jax.random.fold_in(jax.random.fold_in(stream_key, 6), axis_at), (shards_of,), jnp.float32, smallest / len(split), top_value / len(split))
        return jnp.repeat(jnp.exp(steps), dims[axis_at] // shards_of).reshape((-1,) + (1,) * (len(dims) - axis_at - 1))

    loudness = one(*split[0])
    for cut in split[1:]:
        loudness = loudness * one(*cut)
    return loudness


def scatter_about(key, dims, spread, reach, pieces=(), kind=jnp.bfloat16):
    values = spread * jax.random.normal(key, dims, jnp.float32)
    if pieces:
        values = values * levels(key, dims, pieces, -0.22, 0.18)
    return jnp.clip(values, -reach, reach).astype(kind)


def setup_inputs(seed: int = 0, part: int = 0) -> dict:
    splits = jax.random.split(jax.random.key(seed), 9)
    own_keys = jax.random.split(jax.random.fold_in(splits[8], part), 9)
    return {
        "tokens": scatter_about(own_keys[0], (TOKENS, D), 1.0, 6.0, ((0, 2), (1, 4))),
        "norm_gain": jnp.clip(1.0 + 0.18 * jax.random.normal(splits[1], (2, D), jnp.float32), 0.1, 1.9),
        "gate_weight": scatter_about(splits[2], (2, D, FF), D ** -0.5, 0.09375, ((0, 2), (1, 2), (2, 4))),
        "up_weight": scatter_about(splits[3], (2, D, FF), D ** -0.5, 0.09375, ((0, 2), (1, 2), (2, 4))),
        "down_weight": scatter_about(splits[4], (2, FF, D), FF ** -0.5, 0.046875, ((0, 2), (1, 4), (2, 2))),
        "enc_weight": scatter_about(splits[5], (2, D, FEATURES), (2 * D) ** -0.5, 0.0625, ((0, 2), (1, 2), (2, 4))),
        "enc_bias": scatter_about(splits[6], (FEATURES,), 0.5, 3.0, ((0, 4),), jnp.float32),
        "adjoint": scatter_about(own_keys[7], (TOKENS, FEATURES), 1.0, 6.0, ((0, 4), (1, 4))),
    }


def reference(tokens, norm_gain, gate_weight, up_weight, down_weight, enc_weight, enc_bias, adjoint):
    tokens_float = tokens.astype(jnp.float32)
    inverse_rms = lax.rsqrt(lax.optimization_barrier(jnp.mean(tokens_float * tokens_float, axis=-1, keepdims=True)) + 1e-05)
    outputs = []
    for member in range(2):
        normed = (tokens_float * inverse_rms * norm_gain[member][None, :]).astype(jnp.bfloat16)
        gate_acts = jnp.dot(normed, gate_weight[member], preferred_element_type=jnp.float32)
        up_acts = jnp.dot(normed, up_weight[member], preferred_element_type=jnp.float32)
        hidden = (jax.nn.silu(gate_acts) * up_acts).astype(jnp.bfloat16)
        outputs.append(jnp.dot(hidden, down_weight[member], preferred_element_type=jnp.float32).astype(jnp.bfloat16))
    joined = jnp.concatenate(outputs, axis=1)
    pre = jnp.dot(joined, enc_weight.reshape(2 * D, FEATURES), preferred_element_type=jnp.float32) + enc_bias[None, :]
    return (jnp.maximum(pre, 0.0) * adjoint.astype(jnp.float32)).astype(jnp.bfloat16)
```

```python
import functools

import jax
import jax.numpy as jnp
from jax import lax
from jax.experimental import pallas as pl
from jax.experimental.pallas import tpu as pltpu
from jax.sharding import PartitionSpec as P

BF = jnp.bfloat16
F32 = jnp.float32
MESH = pl.DeviceIdType.MESH
VMEM_BYTES = 67_000_000


def tile_of(n, cap):
    best = 128
    for size in range(128, cap + 1, 128):
        if n % size == 0:
            best = size
    return best


def pieces_of(owned, unit):
    n = owned // unit
    if n >= 8:
        weights = (1, 2, 2, 2, 1)
    else:
        weights = (1,) * n
    sizes = [unit * (n * w // sum(weights)) for w in weights]
    sizes[1] += owned - sum(sizes)
    return sizes


def order_of(count):
    out = [("tok_a", 0)]
    for u in range(count + 4):
        steps = [("tok_a", u + 1)] if u + 1 < count else []
        steps += [("tok_b", u), ("tok_c", u), ("gu", u), ("hid", u - 1), ("red", u - 3), ("down", u - 2)]
        steps += [("enc", u - 3), ("mix", u - 3), ("out", u - 4)]
        out += [(name, t) for name, t in steps if 0 <= t < count]
    return out


def kernel(cfg, tok, gain, gate, up, down, enc, bias, adj, result, s):
    sizes, axes = cfg["sizes"], cfg["axes"]
    H, R, M = axes
    count = len(sizes)
    starts = [sum(sizes[:t]) for t in range(count)]
    owned = sum(sizes)
    width, inner = gate.shape[1], gate.shape[2]
    token_width = tok.shape[1]
    features = enc.shape[2]
    per_row = width // token_width
    full = width * R
    h, r, m = lax.axis_index("hid"), lax.axis_index("rows"), lax.axis_index("mp")
    g_tile, d_tile, e_tile, v_tile = cfg["tiles"]

    def hid_at(e):
        return {"hid": lax.rem(h + e, H)}

    def row_at(k):
        return {"rows": lax.rem(r + k, R)}

    def mp_at(d):
        return {"mp": lax.rem(m + d, M)}

    def send(src, dst, name, index, device):
        pltpu.make_async_remote_copy(
            src_ref=src, dst_ref=dst, send_sem=s[name + "_s"].at[index], recv_sem=s[name + "_r"].at[index_of(index, name)],
            device_id=device, device_id_type=MESH,
        ).start()

    def index_of(index, name):
        n = {"zt": H, "xt": R, "xi": R, "mt": M, "mi": M, "gu": R, "hd": R, "rs": H, "ag": H, "pm": M, "px": R}[name]
        return index[:-1] + (n - 2 - index[-1],)

    def done(ref, name, index, device, kind):
        copy = pltpu.make_async_remote_copy(
            src_ref=ref, dst_ref=ref, send_sem=s[name + "_s"].at[index], recv_sem=s[name + "_r"].at[index],
            device_id=device, device_id_type=MESH,
        )
        if kind == "r":
            copy.wait_recv()
        else:
            copy.wait_send()

    rings = {
        "g": (gate, s["wg"], s["wg_m"], g_tile),
        "u": (up, s["wu"], s["wu_m"], g_tile),
        "d": (down, s["wd"], s["wd_m"], d_tile),
        "e": (enc, s["we"], s["we_m"], e_tile),
    }

    def weight(name, tile, slot):
        src, buf, sem, size = rings[name]
        cols = pl.ds(pl.multiple_of(tile * size, size), size)
        return pltpu.make_async_copy(src.at[0, :, cols], buf.at[slot], sem.at[slot])

    def tiles_in(name):
        src, _, _, size = rings[name]
        return src.shape[2] // size

    def stream(names, t, body):
        n = tiles_in(names[0])
        slots = rings[names[0]][1].shape[0]

        def step(i, carry):
            slot = lax.rem(t * n + i, slots)
            for name in names:
                weight(name, i, slot).wait()
            body(i, slot)
            following = i + slots

            def refill():
                for name in names:
                    weight(name, lax.rem(following, n), slot).start()

            if t == count - 1:
                pl.when(following < n)(refill)
            else:
                refill()
            return carry

        lax.fori_loop(0, n, step, 0)

    def prime(names):
        slots = rings[names[0]][1].shape[0]
        for i in range(slots):
            for name in names:
                weight(name, i, i).start()

    def columns(i, size):
        return pl.ds(pl.multiple_of(i * size, size), size)

    def own_rows(t):
        return pl.ds(pl.multiple_of(m * owned + starts[t], 16), sizes[t])

    def tok_start(t):
        rows = pl.ds(starts[t], sizes[t])
        for e in range(H - 1, 0, -1):
            send(tok.at[own_rows(t)], s["zt"].at[h, rows], "zt", (t, e - 1), hid_at(e))
        pltpu.make_async_copy(tok.at[own_rows(t)], s["zt"].at[h, rows], s["zl"].at[t]).start()

    def half(row):
        return pl.ds(row * per_row, per_row)

    def tok_a(t):
        rows = pl.ds(starts[t], sizes[t])
        pltpu.make_async_copy(tok.at[own_rows(t)], s["zt"].at[h, rows], s["zl"].at[t]).wait()
        for e in range(1, H):
            done(s["zt"].at[lax.rem(h + e, H), rows], "zt", (t, e - 1), hid_at(e), "r")
        for k in range(1, R):
            send(
                s["zt"].at[half(lax.rem(r + k, R)), rows], s["raw"].at[R - k, 0, :, rows], "xt", (t, k - 1), row_at(k)
            )
        for d in range(1, M):
            send(s["zt"].at[half(r), rows], s["raw"].at[0, M - d, :, rows], "mt", (t, 0, d - 1), mp_at(d))
        squares = jnp.zeros((sizes[t], 1), F32)
        for e in range(H):
            x = s["zt"][e, rows].astype(F32)
            squares = squares + jnp.sum(x * x, axis=-1, keepdims=True)
        inverse = lax.rsqrt(squares / full + 1e-05)
        s["inv"][0, 0, rows] = jnp.broadcast_to(inverse, (sizes[t], 128))
        for k in range(1, R):
            send(s["inv"].at[0, 0, rows], s["inv"].at[R - k, 0, rows], "xi", (t, k - 1), row_at(k))
        for d in range(1, M):
            send(s["inv"].at[0, 0, rows], s["inv"].at[0, M - d, rows], "mi", (t, 0, d - 1), mp_at(d))

    def tok_b(t):
        rows = pl.ds(starts[t], sizes[t])
        for k in range(1, R):
            done(s["raw"].at[k, 0, :, rows], "xt", (t, k - 1), row_at(k), "r")
            for d in range(1, M):
                send(s["raw"].at[k, 0, :, rows], s["raw"].at[k, M - d, :, rows], "mt", (t, k, d - 1), mp_at(d))
            done(s["inv"].at[k, 0, rows], "xi", (t, k - 1), row_at(k), "r")
            for d in range(1, M):
                send(s["inv"].at[k, 0, rows], s["inv"].at[k, M - d, rows], "mi", (t, k, d - 1), mp_at(d))

    def tok_c(t):
        rows = pl.ds(starts[t], sizes[t])
        base = R * M * starts[t]
        for d in range(M):
            for k in range(R):
                if d:
                    done(s["raw"].at[k, d, :, rows], "mt", (t, k, d - 1), mp_at(d), "r")
                    done(s["inv"].at[k, d, rows], "mi", (t, k, d - 1), mp_at(d), "r")
                inverse = s["inv"][k, d, rows][:, :1]
                at = base + (k * M + d) * sizes[t]
                for b in range(per_row):
                    if k or d:
                        x = s["raw"][k, d, b, rows]
                    else:
                        x = s["zt"][r * per_row + b, rows]
                    cols = pl.ds(pl.multiple_of(r * width + b * token_width, 128), token_width)
                    y = x.astype(F32) * inverse * gain[:, cols]
                    s["normed"][pl.ds(at, sizes[t]), pl.ds(b * token_width, token_width)] = y.astype(BF)

    def gu(t):
        block = M * sizes[t]
        rows = pl.ds(M * starts[t], block)
        lhs = pl.ds(R * M * starts[t], R * block)

        def body(i, slot):
            cols = columns(i, g_tile)
            for which, ring in enumerate(("wg", "wu")):
                acts = jnp.dot(s["normed"][lhs], s[ring][slot], preferred_element_type=F32)
                s["gu_own"][which, rows, cols] = acts[:block]
                for k in range(1, R):
                    s["gu_out"][which, k - 1, rows, cols] = acts[k * block : (k + 1) * block].astype(BF)
            for k in range(1, R):
                send(
                    s["gu_out"].at[:, k - 1, rows, cols], s["gu_in"].at[:, R - k - 1, rows, cols],
                    "gu", (t, k - 1), row_at(k),
                )

        stream(("g", "u"), t, body)

    def hid(t):
        rows = pl.ds(M * starts[t], M * sizes[t])
        for k in range(1, R):
            done(s["gu_in"].at[:, k - 1, rows], "gu", (t, k - 1), row_at(k), "r")

        def step(i, carry):
            cols = columns(i, v_tile)
            sums = []
            for which in range(2):
                total = s["gu_own"][which, rows, cols]
                for k in range(1, R):
                    total = total + s["gu_in"][which, k - 1, rows, cols].astype(F32)
                sums.append(total)
            s["hidden"][0, rows, cols] = (jax.nn.silu(sums[0]) * sums[1]).astype(BF)
            return carry

        lax.fori_loop(0, inner // v_tile, step, 0)
        for k in range(1, R):
            send(s["hidden"].at[0, rows], s["hidden"].at[R - k, rows], "hd", (t, k - 1), row_at(k))

    def quarter(t, who):
        q = R * M * sizes[t] // H
        return pl.ds(pl.multiple_of(R * M * starts[t] + who * q, 16), q)

    def slot_rows(t):
        return pl.ds(R * M * starts[t] // H, R * M * sizes[t] // H)

    def down_(t):
        block = M * sizes[t]
        rows = pl.ds(M * starts[t], block)
        chunk = pl.ds(R * M * starts[t], R * block)
        for k in range(1, R):
            done(s["hidden"].at[k, rows], "hd", (t, k - 1), row_at(k), "r")

        def body(i, slot):
            cols = columns(i, d_tile)
            lhs = s["hidden"][:, rows].reshape(R * block, inner)
            part = jnp.dot(lhs, s["wd"][slot], preferred_element_type=F32)
            s["dn_own"][chunk, cols] = part
            s["dn_out"][chunk, cols] = part.astype(BF)
            for e in range(H - 1, 0, -1):
                send(
                    s["dn_out"].at[quarter(t, lax.rem(h + e, H)), cols], s["dn_in"].at[H - e - 1, slot_rows(t), cols],
                    "rs", (t, e - 1), hid_at(e),
                )

        stream(("d",), t, body)

    def red(t):
        for e in range(1, H):
            done(s["dn_in"].at[e - 1, slot_rows(t)], "rs", (t, e - 1), hid_at(e), "r")
        mine = quarter(t, h)
        total = s["dn_own"][mine]
        for e in range(1, H):
            total = total + s["dn_in"][e - 1, slot_rows(t)].astype(F32)
        s["mlp"][mine] = total.astype(BF)
        for e in range(H - 1, 0, -1):
            send(s["mlp"].at[mine], s["mlp"].at[mine], "ag", (t, e - 1), hid_at(e))

    def enc_(t):
        size = sizes[t]
        rows = pl.ds(starts[t], size)
        chunk = pl.ds(R * M * starts[t], R * M * size)
        for e in range(1, H):
            done(s["mlp"].at[quarter(t, lax.rem(h + e, H))], "ag", (t, e - 1), hid_at(e), "r")

        def body(i, slot):
            cols = columns(i, e_tile)
            part = jnp.dot(s["mlp"][chunk], s["we"][slot], preferred_element_type=F32)
            for k in range(R):
                for d in range(M):
                    at = (k * M + d) * size
                    if d:
                        s["pm_out"][d - 1, k, rows, cols] = part[at : at + size].astype(BF)
                    else:
                        s["pre"][k, rows, cols] = part[at : at + size]
            for d in range(1, M):
                send(
                    s["pm_out"].at[d - 1, :, rows, cols], s["pm_in"].at[M - d - 1, :, rows, cols],
                    "pm", (t, d - 1), mp_at(d),
                )

        stream(("e",), t, body)

    def over_mp(k, rows, cols):
        total = s["pre"][k, rows, cols]
        for d in range(1, M):
            total = total + s["pm_in"][d - 1, k, rows, cols].astype(F32)
        return total

    def mix(t):
        rows = pl.ds(starts[t], sizes[t])
        for d in range(1, M):
            done(s["pm_in"].at[d - 1, :, rows], "pm", (t, d - 1), mp_at(d), "r")

        def step(i, carry):
            cols = columns(i, e_tile)
            for k in range(1, R):
                s["px_out"][k - 1, rows, cols] = over_mp(k, rows, cols).astype(BF)
            return carry

        lax.fori_loop(0, features // e_tile, step, 0)
        for k in range(1, R):
            send(s["px_out"].at[k - 1, rows], s["px_in"].at[R - k - 1, rows], "px", (t, k - 1), row_at(k))

    def out(t):
        rows = pl.ds(starts[t], sizes[t])
        for k in range(1, R):
            done(s["px_in"].at[k - 1, rows], "px", (t, k - 1), row_at(k), "r")

        def step(i, carry):
            cols = columns(i, e_tile)
            total = over_mp(0, rows, cols)
            for k in range(1, R):
                total = total + s["px_in"][k - 1, rows, cols].astype(F32)
            total = total + bias[:, cols]
            scale = s["scale"][rows, cols].astype(F32)
            s["made"][rows, cols] = (jnp.maximum(total, 0.0) * scale).astype(BF)
            return carry

        lax.fori_loop(0, features // e_tile, step, 0)
        pltpu.make_async_copy(s["made"].at[rows], result.at[rows], s["out_m"].at[t]).start()

    barrier = pltpu.get_barrier_semaphore()
    for device in [hid_at(e) for e in range(1, H)] + [row_at(k) for k in range(1, R)] + [mp_at(d) for d in range(1, M)]:
        pl.semaphore_signal(barrier, inc=1, device_id=device, device_id_type=MESH)
    pl.semaphore_wait(barrier, (H - 1) + (R - 1) + (M - 1))

    for t in range(count):
        tok_start(t)
    prime(("g", "u"))
    prime(("d",))
    prime(("e",))
    scale_copy = pltpu.make_async_copy(adj, s["scale"], s["adj_m"].at[0])
    scale_copy.start()

    stages = {
        "tok_a": tok_a, "tok_b": tok_b, "tok_c": tok_c, "gu": gu, "hid": hid, "down": down_,
        "red": red, "enc": enc_, "mix": mix, "out": out,
    }
    scale_seen = False
    for name, t in cfg["order"]:
        if name == "out" and not scale_seen:
            scale_copy.wait()
            scale_seen = True
        stages[name](t)

    for t in range(count):
        rows = pl.ds(starts[t], sizes[t])
        pair_rows = pl.ds(M * starts[t], M * sizes[t])
        for e in range(1, H):
            done(s["zt"].at[0, rows], "zt", (t, e - 1), hid_at(e), "s")
            done(s["dn_in"].at[0, slot_rows(t)], "rs", (t, e - 1), hid_at(e), "s")
            done(s["dn_in"].at[0, slot_rows(t)], "ag", (t, e - 1), hid_at(e), "s")
        for k in range(1, R):
            done(s["raw"].at[k, 0, :, rows], "xt", (t, k - 1), row_at(k), "s")
            done(s["inv"].at[k, 0, rows], "xi", (t, k - 1), row_at(k), "s")
            done(s["gu_out"].at[:, k - 1, pair_rows], "gu", (t, k - 1), row_at(k), "s")
            done(s["hidden"].at[0, pair_rows], "hd", (t, k - 1), row_at(k), "s")
            done(s["px_out"].at[k - 1, rows], "px", (t, k - 1), row_at(k), "s")
        for d in range(1, M):
            for k in range(R):
                done(s["raw"].at[k, 0, :, rows], "mt", (t, k, d - 1), mp_at(d), "s")
                done(s["inv"].at[k, 0, rows], "mi", (t, k, d - 1), mp_at(d), "s")
            done(s["pm_out"].at[d - 1, :, rows], "pm", (t, d - 1), mp_at(d), "s")
        pltpu.make_async_copy(s["made"].at[rows], result.at[rows], s["out_m"].at[t]).wait()


def on_device(
    tokens, norm_gain, gate_weight, up_weight, down_weight, enc_weight, enc_bias, adjoint
):
    H, R, M = (lax.axis_size(a) for a in ("hid", "rows", "mp"))
    _, width, inner = gate_weight.shape
    token_width = tokens.shape[1]
    features = enc_weight.shape[2]
    owned = tokens.shape[0] // M
    unit = max(16, 16 * H // (R * M))
    sizes = pieces_of(owned, unit)
    count = len(sizes)
    per_row = width // token_width
    tiles = (tile_of(inner, 256), tile_of(width, 256), tile_of(features, 256), tile_of(inner, 256))
    cfg = {"sizes": sizes, "axes": (H, R, M), "tiles": tiles, "order": order_of(count)}
    dma = pltpu.SemaphoreType.DMA
    v = pltpu.VMEM
    slots = (3, 2, 3)
    scratch = {
        "zt": v((H, owned, token_width), BF),
        "raw": v((R, M, per_row, owned, token_width), BF),
        "inv": v((R, M, owned, 128), F32),
        "normed": v((R * M * owned, width), BF),
        "gu_own": v((2, M * owned, inner), F32),
        "gu_out": v((2, R - 1, M * owned, inner), BF),
        "gu_in": v((2, R - 1, M * owned, inner), BF),
        "hidden": v((R, M * owned, inner), BF),
        "dn_own": v((R * M * owned, width), F32),
        "dn_out": v((R * M * owned, width), BF),
        "dn_in": v((H - 1, R * M * owned // H, width), BF),
        "mlp": v((R * M * owned, width), BF),
        "pre": v((R, owned, features), F32),
        "pm_out": v((M - 1, R, owned, features), BF),
        "pm_in": v((M - 1, R, owned, features), BF),
        "px_out": v((R - 1, owned, features), BF),
        "px_in": v((R - 1, owned, features), BF),
        "scale": v((owned, features), BF),
        "made": v((owned, features), BF),
        "wg": v((slots[0], width, tiles[0]), BF),
        "wu": v((slots[0], width, tiles[0]), BF),
        "wd": v((slots[1], inner, tiles[1]), BF),
        "we": v((slots[2], width, tiles[2]), BF),
        "wg_m": dma((slots[0],)),
        "wu_m": dma((slots[0],)),
        "wd_m": dma((slots[1],)),
        "we_m": dma((slots[2],)),
        "zl": dma((count,)),
        "adj_m": dma((1,)),
        "out_m": dma((count,)),
    }
    shapes = {
        "zt": (count, H - 1), "rs": (count, H - 1), "ag": (count, H - 1),
        "xt": (count, R - 1), "xi": (count, R - 1), "gu": (count, R - 1), "hd": (count, R - 1), "px": (count, R - 1),
        "mt": (count, R, M - 1), "mi": (count, R, M - 1), "pm": (count, M - 1),
    }
    for name, shape in shapes.items():
        scratch[name + "_s"] = dma(shape)
        scratch[name + "_r"] = dma(shape)
    anywhere = pl.BlockSpec(memory_space=pl.ANY)
    in_vmem = pl.BlockSpec(memory_space=pltpu.VMEM)
    return pl.pallas_call(
        functools.partial(kernel, cfg),
        out_shape=jax.ShapeDtypeStruct((owned, features), BF),
        in_specs=[anywhere, in_vmem, anywhere, anywhere, anywhere, anywhere, in_vmem, anywhere],
        out_specs=anywhere,
        scratch_shapes=[scratch],
        compiler_params=pltpu.CompilerParams(
            collective_id=0, has_side_effects=True, vmem_limit_bytes=VMEM_BYTES
        ),
    )(tokens, norm_gain, gate_weight, up_weight, down_weight, enc_weight, enc_bias[None, :], adjoint)


def solution(mesh):
    placed = (
        P(("groups", "rows"), "hid"),
        P("mp", None),
        P("mp", "rows", "hid"),
        P("mp", "rows", "hid"),
        P("mp", "hid", "rows"),
        P("mp", "rows", "hid"),
        P("hid"),
        P(("groups", "rows", "mp"), "hid"),
    )
    return jax.shard_map(
        on_device,
        mesh=mesh,
        in_specs=placed,
        out_specs=P(("groups", "rows", "mp"), "hid"),
        check_vma=False,
    )
```

```python
import functools

import jax
import jax.numpy as jnp
from jax import lax
from jax.experimental import pallas as pl
from jax.experimental.pallas import tpu as pltpu
from jax.sharding import PartitionSpec as P

BF = jnp.bfloat16
F32 = jnp.float32
MESH = pl.DeviceIdType.MESH
VMEM_BYTES = 67_000_000


def tile_of(n, cap):
    best = 128
    for size in range(128, cap + 1, 128):
        if n % size == 0:
            best = size
    return best


WEIGHTS = (1, 1, 2, 1, 1, 1, 1)
STAGES = {
    "a": "tok_a", "b": "tok_b", "c": "tok_c", "g": "gu", "h": "hid", "d": "down", "r": "red", "e": "enc", "m": "mix", "o": "out",
}
ORDER = (
    "a0", "b0", "a1", "c0", "g0", "a4", "a3", "b1", "c1", "g1", "b3", "b4",
    "a6", "c4", "a2", "a5", "h1", "b6", "b5", "b2", "c2", "c5", "c6", "c3",
    "h0", "g2", "d0", "d1", "g3", "r1", "r0", "h2", "g4", "h3", "g5", "d2",
    "e0", "e1", "r2", "h4", "g6", "h5", "d3", "d4", "r3", "e2", "h6", "r4",
    "m0", "m2", "m1", "d5", "d6", "o0", "e3", "r5", "m3", "o1", "e4", "o3",
    "r6", "m4", "o2", "e5", "m5", "e6", "m6", "o5", "o4", "o6",
)


def pieces_of(owned, unit):
    n = owned // unit
    weights = WEIGHTS if n == sum(WEIGHTS) else (1,) * n
    return [unit * w for w in weights]


def order_of(count):
    if count == len(WEIGHTS):
        return [(STAGES[step[0]], int(step[1:])) for step in ORDER]
    out = [("tok_a", 0)]
    for u in range(count + 4):
        steps = [("tok_a", u + 1)] if u + 1 < count else []
        steps += [("tok_b", u), ("tok_c", u), ("gu", u), ("hid", u - 1), ("red", u - 3), ("down", u - 2)]
        steps += [("enc", u - 3), ("mix", u - 3), ("out", u - 4)]
        out += [(name, t) for name, t in steps if 0 <= t < count]
    return out


def kernel(cfg, tok, gain, gate, up, down, enc, bias, adj, result, s):
    sizes, axes = cfg["sizes"], cfg["axes"]
    H, R, M = axes
    count = len(sizes)
    starts = [sum(sizes[:t]) for t in range(count)]
    owned = sum(sizes)
    width, inner = gate.shape[1], gate.shape[2]
    token_width = tok.shape[1]
    features = enc.shape[2]
    per_row = width // token_width
    full = width * R
    h, r, m = lax.axis_index("hid"), lax.axis_index("rows"), lax.axis_index("mp")
    g_tile, d_tile, e_tile, v_tile = cfg["tiles"]

    def hid_at(e):
        return {"hid": lax.rem(h + e, H)}

    def row_at(k):
        return {"rows": lax.rem(r + k, R)}

    def mp_at(d):
        return {"mp": lax.rem(m + d, M)}

    def send(src, dst, name, index, device):
        pltpu.make_async_remote_copy(
            src_ref=src, dst_ref=dst, send_sem=s[name + "_s"].at[index], recv_sem=s[name + "_r"].at[index_of(index, name)],
            device_id=device, device_id_type=MESH,
        ).start()

    def index_of(index, name):
        n = {"zt": H, "xt": R, "xi": R, "mt": M, "mi": M, "gu": R, "hd": R, "rs": H, "ag": H, "pm": M, "px": R}[name]
        return index[:-1] + (n - 2 - index[-1],)

    def done(ref, name, index, device, kind):
        copy = pltpu.make_async_remote_copy(
            src_ref=ref, dst_ref=ref, send_sem=s[name + "_s"].at[index], recv_sem=s[name + "_r"].at[index],
            device_id=device, device_id_type=MESH,
        )
        if kind == "r":
            copy.wait_recv()
        else:
            copy.wait_send()

    rings = {
        "g": (gate, s["wg"], s["wg_m"], g_tile),
        "u": (up, s["wu"], s["wu_m"], g_tile),
        "d": (down, s["wd"], s["wd_m"], d_tile),
        "e": (enc, s["we"], s["we_m"], e_tile),
    }

    def weight(name, tile, slot):
        src, buf, sem, size = rings[name]
        cols = pl.ds(pl.multiple_of(tile * size, size), size)
        return pltpu.make_async_copy(src.at[0, :, cols], buf.at[slot], sem.at[slot])

    def tiles_in(name):
        src, _, _, size = rings[name]
        return src.shape[2] // size

    def stream(names, t, body):
        n = tiles_in(names[0])
        slots = rings[names[0]][1].shape[0]

        def step(i, carry):
            slot = lax.rem(t * n + i, slots)
            for name in names:
                weight(name, i, slot).wait()
            body(i, slot)
            following = i + slots

            def refill():
                for name in names:
                    weight(name, lax.rem(following, n), slot).start()

            if t == count - 1:
                pl.when(following < n)(refill)
            else:
                refill()
            return carry

        lax.fori_loop(0, n, step, 0)

    def prime(names):
        slots = rings[names[0]][1].shape[0]
        for i in range(slots):
            for name in names:
                weight(name, i, i).start()

    def columns(i, size):
        return pl.ds(pl.multiple_of(i * size, size), size)

    def own_rows(t):
        return pl.ds(pl.multiple_of(m * owned + starts[t], 16), sizes[t])

    def tok_start(t):
        rows = pl.ds(starts[t], sizes[t])
        for e in range(H - 1, 0, -1):
            send(tok.at[own_rows(t)], s["zt"].at[h, rows], "zt", (t, e - 1), hid_at(e))
        pltpu.make_async_copy(tok.at[own_rows(t)], s["zt"].at[h, rows], s["zl"].at[t]).start()

    def half(row):
        return pl.ds(row * per_row, per_row)

    def tok_a(t):
        rows = pl.ds(starts[t], sizes[t])
        pltpu.make_async_copy(tok.at[own_rows(t)], s["zt"].at[h, rows], s["zl"].at[t]).wait()
        for e in range(1, H):
            done(s["zt"].at[lax.rem(h + e, H), rows], "zt", (t, e - 1), hid_at(e), "r")
        for k in range(1, R):
            send(
                s["zt"].at[half(lax.rem(r + k, R)), rows], s["raw"].at[R - k, 0, :, rows], "xt", (t, k - 1), row_at(k)
            )
        for d in range(1, M):
            send(s["zt"].at[half(r), rows], s["raw"].at[0, M - d, :, rows], "mt", (t, 0, d - 1), mp_at(d))
        squares = jnp.zeros((sizes[t], 1), F32)
        for e in range(H):
            x = s["zt"][e, rows].astype(F32)
            squares = squares + jnp.sum(x * x, axis=-1, keepdims=True)
        inverse = lax.rsqrt(squares / full + 1e-05)
        s["inv"][0, 0, rows] = jnp.broadcast_to(inverse, (sizes[t], 128))
        for k in range(1, R):
            send(s["inv"].at[0, 0, rows], s["inv"].at[R - k, 0, rows], "xi", (t, k - 1), row_at(k))
        for d in range(1, M):
            send(s["inv"].at[0, 0, rows], s["inv"].at[0, M - d, rows], "mi", (t, 0, d - 1), mp_at(d))

    def tok_b(t):
        rows = pl.ds(starts[t], sizes[t])
        for k in range(1, R):
            done(s["raw"].at[k, 0, :, rows], "xt", (t, k - 1), row_at(k), "r")
            for d in range(1, M):
                send(s["raw"].at[k, 0, :, rows], s["raw"].at[k, M - d, :, rows], "mt", (t, k, d - 1), mp_at(d))
            done(s["inv"].at[k, 0, rows], "xi", (t, k - 1), row_at(k), "r")
            for d in range(1, M):
                send(s["inv"].at[k, 0, rows], s["inv"].at[k, M - d, rows], "mi", (t, k, d - 1), mp_at(d))

    def tok_c(t):
        rows = pl.ds(starts[t], sizes[t])
        base = R * M * starts[t]
        for d in range(M):
            for k in range(R):
                if d:
                    done(s["raw"].at[k, d, :, rows], "mt", (t, k, d - 1), mp_at(d), "r")
                    done(s["inv"].at[k, d, rows], "mi", (t, k, d - 1), mp_at(d), "r")
                inverse = s["inv"][k, d, rows][:, :1]
                at = base + (k * M + d) * sizes[t]
                for b in range(per_row):
                    if k or d:
                        x = s["raw"][k, d, b, rows]
                    else:
                        x = s["zt"][r * per_row + b, rows]
                    cols = pl.ds(pl.multiple_of(r * width + b * token_width, 128), token_width)
                    y = x.astype(F32) * inverse * gain[:, cols]
                    s["normed"][pl.ds(at, sizes[t]), pl.ds(b * token_width, token_width)] = y.astype(BF)

    def gu(t):
        block = M * sizes[t]
        rows = pl.ds(M * starts[t], block)
        lhs = pl.ds(R * M * starts[t], R * block)

        def body(i, slot):
            cols = columns(i, g_tile)
            for which, ring in enumerate(("wg", "wu")):
                acts = jnp.dot(s["normed"][lhs], s[ring][slot], preferred_element_type=F32)
                s["gu_own"][t % 2, which, pl.ds(0, block), cols] = acts[:block]
                for k in range(1, R):
                    s["gu_out"][which, k - 1, rows, cols] = acts[k * block : (k + 1) * block].astype(BF)
            for k in range(1, R):
                send(
                    s["gu_out"].at[:, k - 1, rows, cols], s["gu_in"].at[:, R - k - 1, rows, cols],
                    "gu", (t, k - 1), row_at(k),
                )

        stream(("g", "u"), t, body)

    def hid(t):
        rows = pl.ds(M * starts[t], M * sizes[t])
        for k in range(1, R):
            done(s["gu_in"].at[:, k - 1, rows], "gu", (t, k - 1), row_at(k), "r")

        def step(i, carry):
            cols = columns(i, v_tile)
            sums = []
            for which in range(2):
                total = s["gu_own"][t % 2, which, pl.ds(0, M * sizes[t]), cols]
                for k in range(1, R):
                    total = total + s["gu_in"][which, k - 1, rows, cols].astype(F32)
                sums.append(total)
            s["hidden"][0, rows, cols] = (jax.nn.silu(sums[0]) * sums[1]).astype(BF)
            return carry

        lax.fori_loop(0, inner // v_tile, step, 0)
        for k in range(1, R):
            send(s["hidden"].at[0, rows], s["hidden"].at[R - k, rows], "hd", (t, k - 1), row_at(k))

    def quarter(t, who):
        q = R * M * sizes[t] // H
        return pl.ds(pl.multiple_of(R * M * starts[t] + who * q, 16), q)

    def slot_rows(t):
        return pl.ds(R * M * starts[t] // H, R * M * sizes[t] // H)

    def down_(t):
        block = M * sizes[t]
        rows = pl.ds(M * starts[t], block)
        chunk = pl.ds(R * M * starts[t], R * block)
        for k in range(1, R):
            done(s["hidden"].at[k, rows], "hd", (t, k - 1), row_at(k), "r")

        def body(i, slot):
            cols = columns(i, d_tile)
            lhs = s["hidden"][:, rows].reshape(R * block, inner)
            part = jnp.dot(lhs, s["wd"][slot], preferred_element_type=F32)
            s["part"][pl.ds(0, R * block)] = part
            s["dn_own"][slot_rows(t), cols] = s["part"][pl.ds(pl.multiple_of(h * (R * block // H), 8), R * block // H)]
            s["dn_out"][chunk, cols] = part.astype(BF)
            for e in range(H - 1, 0, -1):
                send(
                    s["dn_out"].at[quarter(t, lax.rem(h + e, H)), cols], s["dn_in"].at[H - e - 1, slot_rows(t), cols],
                    "rs", (t, e - 1), hid_at(e),
                )

        stream(("d",), t, body)

    def red(t):
        for e in range(1, H):
            done(s["dn_in"].at[e - 1, slot_rows(t)], "rs", (t, e - 1), hid_at(e), "r")
        mine = quarter(t, h)
        total = s["dn_own"][slot_rows(t)]
        for e in range(1, H):
            total = total + s["dn_in"][e - 1, slot_rows(t)].astype(F32)
        s["mlp"][mine] = total.astype(BF)
        for e in range(H - 1, 0, -1):
            send(s["mlp"].at[mine], s["mlp"].at[mine], "ag", (t, e - 1), hid_at(e))

    def enc_(t):
        size = sizes[t]
        rows = pl.ds(starts[t], size)
        chunk = pl.ds(R * M * starts[t], R * M * size)
        for e in range(1, H):
            done(s["mlp"].at[quarter(t, lax.rem(h + e, H))], "ag", (t, e - 1), hid_at(e), "r")

        def body(i, slot):
            cols = columns(i, e_tile)
            part = jnp.dot(s["mlp"][chunk], s["we"][slot], preferred_element_type=F32)
            for k in range(R):
                for d in range(M):
                    at = (k * M + d) * size
                    if d:
                        s["pm_out"][d - 1, k, rows, cols] = part[at : at + size].astype(BF)
                    else:
                        s["pre"][t % 3, k, pl.ds(0, size), cols] = part[at : at + size]
            for d in range(1, M):
                send(
                    s["pm_out"].at[d - 1, :, rows, cols], s["pm_in"].at[M - d - 1, :, rows, cols],
                    "pm", (t, d - 1), mp_at(d),
                )

        stream(("e",), t, body)

    def over_mp(t, k, rows, cols):
        total = s["pre"][t % 3, k, pl.ds(0, sizes[t]), cols]
        for d in range(1, M):
            total = total + s["pm_in"][d - 1, k, rows, cols].astype(F32)
        return total

    def mix(t):
        rows = pl.ds(starts[t], sizes[t])
        for d in range(1, M):
            done(s["pm_in"].at[d - 1, :, rows], "pm", (t, d - 1), mp_at(d), "r")

        def step(i, carry):
            cols = columns(i, e_tile)
            for k in range(1, R):
                s["px_out"][k - 1, rows, cols] = over_mp(t, k, rows, cols).astype(BF)
            return carry

        lax.fori_loop(0, features // e_tile, step, 0)
        for k in range(1, R):
            send(s["px_out"].at[k - 1, rows], s["px_in"].at[R - k - 1, rows], "px", (t, k - 1), row_at(k))

    def out(t):
        rows = pl.ds(starts[t], sizes[t])
        for k in range(1, R):
            done(s["px_in"].at[k - 1, rows], "px", (t, k - 1), row_at(k), "r")

        def step(i, carry):
            cols = columns(i, e_tile)
            total = over_mp(t, 0, rows, cols)
            for k in range(1, R):
                total = total + s["px_in"][k - 1, rows, cols].astype(F32)
            total = total + bias[:, cols]
            scale = s["scale"][rows, cols].astype(F32)
            s["made"][rows, cols] = (jnp.maximum(total, 0.0) * scale).astype(BF)
            return carry

        lax.fori_loop(0, features // e_tile, step, 0)
        pltpu.make_async_copy(s["made"].at[rows], result.at[rows], s["out_m"].at[t]).start()

    barrier = pltpu.get_barrier_semaphore()
    for device in [hid_at(e) for e in range(1, H)] + [row_at(k) for k in range(1, R)] + [mp_at(d) for d in range(1, M)]:
        pl.semaphore_signal(barrier, inc=1, device_id=device, device_id_type=MESH)
    pl.semaphore_wait(barrier, (H - 1) + (R - 1) + (M - 1))

    for t in range(count):
        tok_start(t)
    prime(("g", "u"))
    prime(("d",))
    prime(("e",))
    scale_copy = pltpu.make_async_copy(adj, s["scale"], s["adj_m"].at[0])
    scale_copy.start()

    stages = {
        "tok_a": tok_a, "tok_b": tok_b, "tok_c": tok_c, "gu": gu, "hid": hid, "down": down_,
        "red": red, "enc": enc_, "mix": mix, "out": out,
    }
    scale_seen = False
    for name, t in cfg["order"]:
        if name == "out" and not scale_seen:
            scale_copy.wait()
            scale_seen = True
        stages[name](t)

    for t in range(count):
        rows = pl.ds(starts[t], sizes[t])
        pair_rows = pl.ds(M * starts[t], M * sizes[t])
        for e in range(1, H):
            done(s["zt"].at[0, rows], "zt", (t, e - 1), hid_at(e), "s")
            done(s["dn_in"].at[0, slot_rows(t)], "rs", (t, e - 1), hid_at(e), "s")
            done(s["dn_in"].at[0, slot_rows(t)], "ag", (t, e - 1), hid_at(e), "s")
        for k in range(1, R):
            done(s["raw"].at[k, 0, :, rows], "xt", (t, k - 1), row_at(k), "s")
            done(s["inv"].at[k, 0, rows], "xi", (t, k - 1), row_at(k), "s")
            done(s["gu_out"].at[:, k - 1, pair_rows], "gu", (t, k - 1), row_at(k), "s")
            done(s["hidden"].at[0, pair_rows], "hd", (t, k - 1), row_at(k), "s")
            done(s["px_out"].at[k - 1, rows], "px", (t, k - 1), row_at(k), "s")
        for d in range(1, M):
            for k in range(R):
                done(s["raw"].at[k, 0, :, rows], "mt", (t, k, d - 1), mp_at(d), "s")
                done(s["inv"].at[k, 0, rows], "mi", (t, k, d - 1), mp_at(d), "s")
            done(s["pm_out"].at[d - 1, :, rows], "pm", (t, d - 1), mp_at(d), "s")
        pltpu.make_async_copy(s["made"].at[rows], result.at[rows], s["out_m"].at[t]).wait()


def on_device(
    tokens, norm_gain, gate_weight, up_weight, down_weight, enc_weight, enc_bias, adjoint
):
    H, R, M = (lax.axis_size(a) for a in ("hid", "rows", "mp"))
    _, width, inner = gate_weight.shape
    token_width = tokens.shape[1]
    features = enc_weight.shape[2]
    owned = tokens.shape[0] // M
    unit = max(16, 16 * H // (R * M))
    sizes = pieces_of(owned, unit)
    count, most = len(sizes), max(sizes)
    per_row = width // token_width
    tiles = (tile_of(inner, 256), tile_of(width, 256), tile_of(features, 256), tile_of(inner, 256))
    cfg = {"sizes": sizes, "axes": (H, R, M), "tiles": tiles, "order": order_of(count)}
    dma = pltpu.SemaphoreType.DMA
    v = pltpu.VMEM
    slots = [min(a, b // c) for a, b, c in zip((4, 4, 6), (inner, width, features), tiles)]
    scratch = {
        "zt": v((H, owned, token_width), BF),
        "raw": v((R, M, per_row, owned, token_width), BF),
        "inv": v((R, M, owned, 128), F32),
        "normed": v((R * M * owned, width), BF),
        "gu_own": v((2, 2, M * most, inner), F32),
        "gu_out": v((2, R - 1, M * owned, inner), BF),
        "gu_in": v((2, R - 1, M * owned, inner), BF),
        "hidden": v((R, M * owned, inner), BF),
        "dn_own": v((R * M * owned // H, width), F32),
        "part": v((R * M * most, tiles[1]), F32),
        "dn_out": v((R * M * owned, width), BF),
        "dn_in": v((H - 1, R * M * owned // H, width), BF),
        "mlp": v((R * M * owned, width), BF),
        "pre": v((3, R, most, features), F32),
        "pm_out": v((M - 1, R, owned, features), BF),
        "pm_in": v((M - 1, R, owned, features), BF),
        "px_out": v((R - 1, owned, features), BF),
        "px_in": v((R - 1, owned, features), BF),
        "scale": v((owned, features), BF),
        "made": v((owned, features), BF),
        "wg": v((slots[0], width, tiles[0]), BF),
        "wu": v((slots[0], width, tiles[0]), BF),
        "wd": v((slots[1], inner, tiles[1]), BF),
        "we": v((slots[2], width, tiles[2]), BF),
        "wg_m": dma((slots[0],)),
        "wu_m": dma((slots[0],)),
        "wd_m": dma((slots[1],)),
        "we_m": dma((slots[2],)),
        "zl": dma((count,)),
        "adj_m": dma((1,)),
        "out_m": dma((count,)),
    }
    shapes = {
        "zt": (count, H - 1), "rs": (count, H - 1), "ag": (count, H - 1),
        "xt": (count, R - 1), "xi": (count, R - 1), "gu": (count, R - 1), "hd": (count, R - 1), "px": (count, R - 1),
        "mt": (count, R, M - 1), "mi": (count, R, M - 1), "pm": (count, M - 1),
    }
    for name, shape in shapes.items():
        scratch[name + "_s"] = dma(shape)
        scratch[name + "_r"] = dma(shape)
    anywhere = pl.BlockSpec(memory_space=pl.ANY)
    in_vmem = pl.BlockSpec(memory_space=pltpu.VMEM)
    return pl.pallas_call(
        functools.partial(kernel, cfg),
        out_shape=jax.ShapeDtypeStruct((owned, features), BF),
        in_specs=[anywhere, in_vmem, anywhere, anywhere, anywhere, anywhere, in_vmem, anywhere],
        out_specs=anywhere,
        scratch_shapes=[scratch],
        compiler_params=pltpu.CompilerParams(
            collective_id=0, has_side_effects=True, vmem_limit_bytes=VMEM_BYTES
        ),
    )(tokens, norm_gain, gate_weight, up_weight, down_weight, enc_weight, enc_bias[None, :], adjoint)


def solution(mesh):
    placed = (
        P(("groups", "rows"), "hid"),
        P("mp", None),
        P("mp", "rows", "hid"),
        P("mp", "rows", "hid"),
        P("mp", "hid", "rows"),
        P("mp", "rows", "hid"),
        P("hid"),
        P(("groups", "rows", "mp"), "hid"),
    )
    return jax.shard_map(
        on_device,
        mesh=mesh,
        in_specs=placed,
        out_specs=P(("groups", "rows", "mp"), "hid"),
        check_vma=False,
    )
```
